32 devices in a mesh: section: 4 (over x, core), expert: 8 (over z, y).
Axes of the slice: x: 2, y: 2, z: 4, core: 2. Of those that a mesh axis runs over, the one named last changes fastest.
Arguments:
- layer_input: bfloat16 [2, 4, 1024, 2048], P(None, 'section', 'expert'), may hold values from -48 to 48
- entering: bfloat16 [4, 1024, 2048], P('section', 'expert'), may hold values from -6 to 6
- fresh: bfloat16 [1, 1024, 2048], P(None, 'expert'), may hold values from -6 to 6
- routes: int32 [2, 4, 1024, 2], P(None, 'section', 'expert'), may hold values from 0 to 7, all different within a row; in each aligned block of 128 rows (0 to 127, 128 to 255, ..., all dimensions but the last counted through in order) at most 48 rows name the same one
- gate_weights: bfloat16 [2, 4, 1024, 2], P(None, 'section', 'expert'), may hold values from 0.019897461 to 0.5
- norm_gain: float32 [4, 2048], P('section'), may hold values from 0.3 to 3
- w_gate: bfloat16 [4, 8, 2048, 768], P('section', 'expert'), may hold values from -0.125 to 0.125
- w_up: bfloat16 [4, 8, 2048, 768], P('section', 'expert'), may hold values from -0.125 to 0.125
- w_down: bfloat16 [4, 8, 768, 2048], P('section', 'expert'), may hold values from -0.21875 to 0.21875
Outputs:
- produced: bfloat16 [2, 4, 1024, 2048], P(None, 'section', 'expert')
The draws below stay inside these ranges and needn't reach their ends.
Inputs may be any that keep to these rules, and one draw needn't show every extreme that they name: `routes`: each row names 2 different experts; in each aligned block of 128 rows no expert is named more than 48 times, a bound that some block reaches.
All inputs are finite; a program needn't handle non-finite values.
Results may differ from the reference program's by a relative error of at most 0.0052.
Values may be sent and summed in bfloat16 or wider, within the bound.
No kernel may reach another device: no remote copies, remote signals or barrier semaphores. Data moves between devices by JAX's collectives and lax.ppermute only.
A program may use at most 128 MiB of HBM per device.

```python
import math
import jax
import jax.numpy as jnp
import numpy as np
from jax import lax

D = 2048
FFE = 768
TOPK = 2
TICKS = 2
TOK_DEV = 128
SECTIONS = 4
EXPERTS = 8
TOKENS = 1024
SLOTS = 48
N_EXPERT = 8


def draw_layer_input(key, part):
    base_key, row_key, column_key = jax.random.split(key, 3)
    shape_all = (TICKS, SECTIONS, TOKENS, D)
    base_values = jnp.clip(jax.random.normal(base_key, shape_all, jnp.float32), -4.0, 4.0)
    row_scale = jnp.exp(jax.random.uniform(row_key, (TICKS, SECTIONS, TOKENS, 1), jnp.float32, math.log(0.3), math.log(3.0)))
    column_scale = jnp.exp(jax.random.uniform(column_key, (1, 1, 1, D), jnp.float32, math.log(0.4), math.log(4.0)))
    return (base_values * row_scale * column_scale).astype(jnp.bfloat16)


def level_of(key, dims, cuts, least, high):
    def one(axis_at, blocks):
        draws = jax.random.uniform(jax.random.fold_in(jax.random.fold_in(key, 6), axis_at), (blocks,), jnp.float32, least / len(cuts), high / len(cuts))
        return jnp.repeat(jnp.exp(draws), dims[axis_at] // blocks).reshape((-1,) + (1,) * (len(dims) - axis_at - 1))

    loudness = one(*cuts[0])
    for cut in cuts[1:]:
        loudness = loudness * one(*cut)
    return loudness


def routed_block(key, own, number, rows, number_of, top, reach, skew):
    ranking = jax.random.permutation(key, number_of)
    heavy_load, common = load_shares(number_of, rows * top, reach, skew, True), load_shares(number_of, rows * top, reach, skew, False)
    places = jnp.arange(number_of)

    def named(tallies, offset_by):
        used = int((tallies > 0).sum())
        fixed = max(1, used // 4)
        moved = fixed + (places - fixed + offset_by * (used - fixed)) % max(1, number_of - fixed)
        return jnp.zeros((number_of,), jnp.int32).at[ranking[jnp.where(places < fixed, places, moved)]].set(jnp.asarray(tallies, jnp.int32))

    tallies = jnp.where(number % 4 == 0, named(heavy_load, number // 4), named(common, number - number // 4 - 1))
    mixed = jax.random.permutation(jax.random.fold_in(own, 3), number_of)
    donor, receiver = mixed[0:number_of // 2 * 2:2], mixed[1:number_of // 2 * 2:2]
    margin = jnp.minimum(tallies[donor] - 1, reach - tallies[receiver]) // 2
    margin = jnp.where((donor == ranking[0]) | (receiver == ranking[0]) | (tallies[receiver] == 0), 0, jnp.maximum(margin, 0))
    moved = jax.random.randint(jax.random.fold_in(own, 4), (number_of // 2,), 0, 1 << 20) % (margin + 1)
    tallies = tallies.at[donor].add(-moved).at[receiver].add(moved)
    items = jnp.searchsorted(jnp.cumsum(tallies), jnp.arange(rows * top), side="right").astype(jnp.int32)
    grid = items.reshape(top, rows).T
    grid = grid[jax.random.permutation(jax.random.fold_in(own, 1), rows)]
    offset_by = jax.random.randint(jax.random.fold_in(own, 2), (rows, 1), 0, top)
    return jnp.take_along_axis(grid, (jnp.arange(top)[None, :] + offset_by) % top, axis=1)


def load_shares(number_of, total, reach, lean, full):
    portions = [(1 << 20) // math.isqrt(grade ** lean) + 1 for grade in range(1, number_of + 1)]
    largest = reach if full else min(reach, max(-(-total // number_of), total * portions[0] // sum(portions)))
    least = 1 if total - largest >= number_of - 1 else 0
    holding, spare = [largest] + [least] * (number_of - 1), total - largest - least * (number_of - 1)
    while spare > 0:
        movable = [i for i in range(1, number_of) if holding[i] < largest] or [i for i in range(1, number_of) if holding[i] < reach]
        mass, budget = sum([portions[i] for i in movable]), spare
        for i in movable:
            more = min(reach - holding[i], max(1, budget * portions[i] // mass), spare)
            holding[i] = holding[i] + more
            spare = spare - more
    return np.array(holding)


def noise(own_key, extent, spread, reach, cuts=(), held_as=jnp.bfloat16):
    values = jax.random.normal(own_key, extent, jnp.float32) * spread
    if len(cuts) > 0:
        values = level_of(own_key, extent, cuts, -0.22, 0.18) * values
    return jnp.clip(values, min=-reach, max=reach).astype(held_as)


def setup_inputs(seed: int = 0) -> dict:
    keys = jax.random.split(jax.random.key(seed), 10)
    layer_input = draw_layer_input(jax.random.fold_in(keys[9], 71), 0)
    entering = noise(keys[1], (SECTIONS, TOKENS, D), 1.0, 6.0, ((0, 4), (1, 8)))
    fresh = noise(keys[2], (TICKS - 1, TOKENS, D), 1.0, 6.0, ((1, 8),))
    routes_keys = jax.random.split(jax.random.fold_in(keys[3], 1), TICKS * SECTIONS * TOKENS // TOK_DEV)
    routes_turns = jax.random.permutation(jax.random.fold_in(keys[3], 3), TICKS * SECTIONS * TOKENS // TOK_DEV)
    routes = jax.vmap(lambda own, number: routed_block(jax.random.fold_in(keys[3], 2), own, number, TOK_DEV, EXPERTS, TOPK, SLOTS, 2))(routes_keys, routes_turns).reshape((TICKS, SECTIONS, TOKENS, TOPK))
    gate_weights = jnp.clip(jnp.exp(math.log(0.5) - 3.224016 * jax.random.uniform(keys[4], (TICKS, SECTIONS, TOKENS, TOPK), jnp.float32) ** level_of(keys[4], (TICKS, SECTIONS, TOKENS, TOPK), ((1, 4), (2, 8)), -0.2, 0.2)), 0.019897461, 0.5).astype(jnp.bfloat16)
    norm_gain = jnp.clip(jnp.exp(math.log(3.0) - 2.3025851 * jax.random.uniform(keys[5], (SECTIONS, D), jnp.float32) ** level_of(keys[5], (SECTIONS, D), ((0, 4),), -0.2, 0.2)), 0.3, 3.0)
    w_gate = noise(keys[6], (SECTIONS, EXPERTS, D, FFE), D ** -0.5, 0.125, ((0, 4), (1, 8)))
    w_up = noise(keys[7], (SECTIONS, EXPERTS, D, FFE), D ** -0.5, 0.125, ((0, 4), (1, 8)))
    w_down = noise(keys[8], (SECTIONS, EXPERTS, FFE, D), FFE ** -0.5, 0.21875, ((0, 4), (1, 8)))
    return {"layer_input": layer_input, "entering": entering, "fresh": fresh, "routes": routes, "gate_weights": gate_weights, "norm_gain": norm_gain, "w_gate": w_gate, "w_up": w_up, "w_down": w_down}


def contract_last(left, right):
    return lax.dot_general(left, right, (((1,), (1,)), ((), ())), preferred_element_type=jnp.float32)

def expert_backward(normed_rows, scaled_rows, gate_matrix, up_matrix, down_matrix):
    pre_gate = jnp.dot(normed_rows, gate_matrix, preferred_element_type=jnp.float32)
    pre_up = jnp.dot(normed_rows, up_matrix, preferred_element_type=jnp.float32)
    hidden_grad = contract_last(scaled_rows, down_matrix)
    sigmoid = jax.nn.sigmoid(pre_gate)
    gate_grad = (hidden_grad * pre_up * sigmoid * (1.0 + pre_gate * (1.0 - sigmoid))).astype(jnp.bfloat16)
    up_grad = (hidden_grad * pre_gate * sigmoid).astype(jnp.bfloat16)
    summed = contract_last(gate_grad, gate_matrix) + contract_last(up_grad, up_matrix)
    return summed.astype(jnp.bfloat16)

def layer_backward(layer_rows, incoming, route_rows, gate_rows, gain_row, gate_stack, up_stack, down_stack):
    xfloat = layer_rows.astype(jnp.float32)
    inverse = lax.rsqrt(lax.optimization_barrier(jnp.mean(xfloat * xfloat, axis=1, keepdims=True)) + 1e-05)
    normed = (xfloat * inverse * gain_row).astype(jnp.bfloat16)
    scaled = (gate_rows.astype(jnp.float32)[:, :, None] * incoming.astype(jnp.float32)[:, None, :]).astype(jnp.bfloat16)
    scaled = scaled.reshape(-1, D)
    flat_routes = route_rows.reshape(-1).astype(jnp.int32)
    assignments = flat_routes.shape[0]
    limit_rows = N_EXPERT * SLOTS

    def one_expert(collected, expert):
        picked = jnp.nonzero(flat_routes == expert, size=limit_rows, fill_value=assignments)[0].astype(jnp.int32)
        safe_index = jnp.minimum(picked, assignments - 1).astype(jnp.int32)
        result = expert_backward(normed[safe_index // TOPK], scaled[safe_index], gate_stack[expert], up_stack[expert], down_stack[expert])
        return (collected.at[picked].set(result, mode='drop'), None)
    collected, unused = lax.scan(one_expert, jnp.zeros((assignments, D), jnp.bfloat16), jnp.arange(EXPERTS, dtype=jnp.int32))
    normed_grad = lax.optimization_barrier(jnp.sum(collected.reshape(-1, TOPK, D).astype(jnp.float32), axis=1))
    weighted = gain_row * normed_grad
    project = lax.optimization_barrier(jnp.mean(xfloat * weighted, axis=1, keepdims=True))
    result = incoming.astype(jnp.float32) + inverse * weighted - xfloat * inverse ** 3 * project
    return result.astype(jnp.bfloat16)

def reference(layer_input, entering, fresh, routes, gate_weights, norm_gain, w_gate, w_up, w_down):
    produced = []
    for tick_index in range(TICKS):
        current = []
        for section_index in range(SECTIONS):
            if tick_index == 0:
                incoming = entering[section_index]
            elif section_index == SECTIONS - 1:
                incoming = fresh[tick_index - 1]
            else:
                incoming = produced[tick_index - 1][section_index + 1]
            current.append(layer_backward(layer_input[tick_index, section_index], incoming, routes[tick_index, section_index], gate_weights[tick_index, section_index], norm_gain[section_index], w_gate[section_index], w_up[section_index], w_down[section_index]))
        produced.append(current)
    return jnp.stack([jnp.stack(row_list, axis=0) for row_list in produced], axis=0)
```

```python
import jax
import jax.numpy as jnp
from jax import lax
from jax.sharding import Mesh, PartitionSpec as P

TICKS = 2
TOPK = 2
BOTH = ("quad", "half")


def contract_last(left, right):
    return lax.dot_general(
        left, right, (((1,), (1,)), ((), ())), preferred_element_type=jnp.float32
    )


def after(value, *others):
    return lax.optimization_barrier((value,) + others)[0]


def swap(value):
    return lax.ppermute(value, "half", [(0, 1), (1, 0)])


def positions(routes, quads, slots):
    tokens, topk = routes.shape
    experts = 2 * quads
    flat = routes.reshape(-1)
    onehot = (flat[:, None] == jnp.arange(experts, dtype=jnp.int32)[None, :]).astype(jnp.bfloat16)
    count = flat.shape[0]
    row = lax.broadcasted_iota(jnp.int32, (count, count), 0)
    col = lax.broadcasted_iota(jnp.int32, (count, count), 1)
    earlier = jnp.dot(
        (col < row).astype(jnp.bfloat16), onehot, preferred_element_type=jnp.float32
    )
    rank = jnp.sum(earlier * onehot.astype(jnp.float32), axis=1).astype(jnp.int32)
    place = ((flat % quads) * 2 + flat // quads) * slots + rank
    return place.reshape(tokens, topk)


def select(place, slot_of):
    hit = place[:, 0][None, :] == slot_of[:, None]
    for k in range(1, TOPK):
        hit = hit | (place[:, k][None, :] == slot_of[:, None])
    return hit.astype(jnp.bfloat16)


def gate_of(place, gates, slot_of):
    total = jnp.zeros(slot_of.shape, jnp.float32)
    for k in range(TOPK):
        hit = place[:, k][None, :] == slot_of[:, None]
        total = total + jnp.sum(jnp.where(hit, gates[:, k].astype(jnp.float32)[None, :], 0.0), axis=1)
    return total


def local(layer_input, entering, fresh, routes, gate_weights, norm_gain, w_gate, w_up, w_down):
    quads = lax.axis_size("quad")
    experts = 2 * quads
    tokens, width = layer_input.shape[2], layer_input.shape[3]
    slots = max(2, min(tokens, 3 * tokens * TOPK // (2 * experts)))
    rows = experts * slots
    half_here = lax.axis_index("half")
    section_here = lax.axis_index("section")
    section_last = lax.axis_size("section") - 1
    gain = norm_gain[0]
    gate_matrix, up_matrix, down_matrix = w_gate[0, 0], w_up[0, 0], w_down[0, 0]

    def norm(t):
        xfloat = layer_input[t, 0].astype(jnp.float32)
        inverse = lax.rsqrt(jnp.mean(xfloat * xfloat, axis=1, keepdims=True) + 1e-05)
        return (xfloat * inverse * gain).astype(jnp.bfloat16), inverse

    def incoming_pack(values, place, gates):
        slot_of = jnp.arange(rows, dtype=jnp.int32)
        packed = jnp.dot(select(place, slot_of), values, preferred_element_type=jnp.float32)
        return (packed * gate_of(place, gates, slot_of)[:, None]).astype(jnp.bfloat16)

    index = jnp.arange(rows, dtype=jnp.int32)
    source_half = (index // slots) % 2
    own_row = source_half == half_here
    wanted = (index // (2 * slots) * 2 + half_here) * slots + index % slots

    def pair_select(own_place, mirror_place):
        own = select(own_place, jnp.where(own_row, wanted, -1))
        mirror = select(mirror_place, jnp.where(own_row, -1, wanted))
        return jnp.concatenate([own, mirror], axis=1)

    def pair_gate(own_place, own_gates, mirror_place, mirror_gates):
        own = gate_of(own_place, own_gates, jnp.where(own_row, wanted, -1))
        mirror = gate_of(mirror_place, mirror_gates, jnp.where(own_row, -1, wanted))
        return own + mirror

    def quad_exchange(packed):
        return lax.all_to_all(
            packed.reshape(quads, 2 * slots, width), "quad", split_axis=0, concat_axis=0, tiled=True
        ).reshape(rows, width)

    def full_exchange(packed):
        return lax.all_to_all(
            packed.reshape(experts, slots, width), BOTH, split_axis=0, concat_axis=0, tiled=True
        ).reshape(rows, width)

    def hidden(normed_rows):
        pre_gate = jnp.dot(normed_rows, gate_matrix, preferred_element_type=jnp.float32)
        pre_up = jnp.dot(normed_rows, up_matrix, preferred_element_type=jnp.float32)
        return pre_gate, pre_up

    def backward(pre_gate, pre_up, hidden_grad):
        sigmoid = jax.nn.sigmoid(pre_gate)
        gate_grad = (
            hidden_grad * pre_up * sigmoid * (1.0 + pre_gate * (1.0 - sigmoid))
        ).astype(jnp.bfloat16)
        up_grad = (hidden_grad * pre_gate * sigmoid).astype(jnp.bfloat16)
        summed = contract_last(gate_grad, gate_matrix) + contract_last(up_grad, up_matrix)
        return summed.astype(jnp.bfloat16)

    def combine(t, incoming, returned, place, inverse):
        chosen = select(place, jnp.arange(rows, dtype=jnp.int32))
        normed_grad = lax.dot_general(
            chosen, returned, (((0,), (0,)), ((), ())), preferred_element_type=jnp.float32
        )
        xfloat = layer_input[t, 0].astype(jnp.float32)
        weighted = gain * normed_grad
        project = jnp.mean(xfloat * weighted, axis=1, keepdims=True)
        return (
            incoming.astype(jnp.float32) + inverse * weighted - xfloat * inverse**3 * project
        ).astype(jnp.bfloat16)

    place = [positions(routes[t, 0], quads, slots) for t in range(TICKS)]
    gates = [gate_weights[t, 0] for t in range(TICKS)]

    grad_mirror = swap(entering[0])
    place_mirror = swap(jnp.stack(place, axis=0))
    gates_mirror = swap(gates[0])
    normed0, inverse0 = norm(0)
    normed1, inverse1 = norm(1)
    normed0_mirror = swap(after(normed0, grad_mirror))
    normed1_mirror = swap(after(normed1, normed0_mirror))

    pair0 = pair_select(place[0], place_mirror[0])
    pair1 = pair_select(place[1], place_mirror[1])
    scale0 = pair_gate(place[0], gates[0], place_mirror[0], gates_mirror)

    both = jnp.concatenate([entering[0], grad_mirror], axis=0)
    packed = jnp.dot(pair0, both, preferred_element_type=jnp.float32)
    scaled0 = quad_exchange((packed * scale0[:, None]).astype(jnp.bfloat16))
    hidden_grad0 = contract_last(scaled0, down_matrix)

    both = jnp.concatenate([normed0, normed0_mirror], axis=0)
    rows0 = quad_exchange(jnp.dot(pair0, both, preferred_element_type=jnp.bfloat16))
    pre_gate0, pre_up0 = hidden(rows0)
    computed0 = backward(pre_gate0, pre_up0, hidden_grad0)
    returned0 = full_exchange(computed0)

    both = jnp.concatenate([normed1, normed1_mirror], axis=0)
    packed1 = jnp.dot(pair1, both, preferred_element_type=jnp.bfloat16)
    rows1 = quad_exchange(after(packed1, returned0))
    result0 = combine(0, entering[0], returned0, place[0], inverse0)

    length = section_last + 1
    arrived = lax.ppermute(result0, "section", [(i, i - 1) for i in range(1, length)])
    incoming = jnp.where(section_here == section_last, fresh[0], arrived)
    scaled1 = full_exchange(incoming_pack(incoming, place[1], gates[1]))
    pre_gate1, pre_up1 = hidden(rows1)
    computed1 = backward(pre_gate1, pre_up1, contract_last(scaled1, down_matrix))
    returned1 = full_exchange(computed1)
    result1 = combine(1, incoming, returned1, place[1], inverse1)
    return jnp.stack([result0, result1], axis=0)[:, None]


def solution(mesh):
    sections, experts = mesh.shape["section"], mesh.shape["expert"]
    split = Mesh(mesh.devices.reshape(sections, 2, experts // 2), ("section", "half", "quad"))
    expert = ("half", "quad")
    in_specs = (
        P(None, "section", expert, None),
        P("section", expert, None),
        P(None, expert, None),
        P(None, "section", expert, None),
        P(None, "section", expert, None),
        P("section", None),
        P("section", expert, None, None),
        P("section", expert, None, None),
        P("section", expert, None, None),
    )
    out_specs = P(None, "section", expert, None)
    return jax.shard_map(local, mesh=split, in_specs=in_specs, out_specs=out_specs, check_vma=False)
```

```python
import functools

import jax
import jax.numpy as jnp
from jax import lax
from jax.experimental import pallas as pl
from jax.experimental.pallas import tpu as pltpu
from jax.sharding import Mesh, PartitionSpec as P

TICKS = 2
TOPK = 2
BOTH = ("quad", "half")


def contract_last(left, right):
    return lax.dot_general(
        left, right, (((1,), (1,)), ((), ())), preferred_element_type=jnp.float32
    )


def piece(size, want):
    return want if size % want == 0 else size


def pre_kernel(rows_ref, gate_ref, up_ref, pre_gate_ref, pre_up_ref):
    rows = rows_ref[...]
    pre_gate_ref[...] = jnp.dot(rows, gate_ref[...], preferred_element_type=jnp.float32)
    pre_up_ref[...] = jnp.dot(rows, up_ref[...], preferred_element_type=jnp.float32)


def pre_activations(rows, gate_matrix, up_matrix):
    count, width = rows.shape
    hidden = gate_matrix.shape[1]
    part = piece(hidden, 256)
    weight = pl.BlockSpec((width, part), lambda i: (0, i))
    out = pl.BlockSpec((count, part), lambda i: (0, i))
    return pl.pallas_call(
        pre_kernel,
        grid=(hidden // part,),
        in_specs=[pl.BlockSpec((count, width), lambda i: (0, 0)), weight, weight],
        out_specs=[out, out],
        out_shape=[jax.ShapeDtypeStruct((count, hidden), jnp.float32)] * 2,
        compiler_params=pltpu.CompilerParams(vmem_limit_bytes=24 * 2**20),
        cost_estimate=pl.CostEstimate(
            flops=4 * count * width * hidden,
            bytes_accessed=4 * width * hidden + 2 * count * width + 8 * count * hidden,
            transcendentals=0,
        ),
        name="pre_activations",
    )(rows, gate_matrix, up_matrix)


def backward_kernel(
    parts, scaled_ref, pre_gate_ref, pre_up_ref, down_ref, gate_ref, up_ref, out_ref, gate_grad, up_grad
):
    step = pl.program_id(0)

    @pl.when(step < parts)
    def _():
        hidden_grad = contract_last(scaled_ref[...], down_ref[...])
        pre_gate = pre_gate_ref[...]
        sigmoid = 1.0 / (1.0 + jnp.exp(-pre_gate))
        both = hidden_grad * sigmoid
        gate_grad[step] = (both * pre_up_ref[...] * (1.0 + pre_gate * (1.0 - sigmoid))).astype(
            jnp.bfloat16
        )
        up_grad[step] = (both * pre_gate).astype(jnp.bfloat16)

    @pl.when(step >= parts)
    def _():
        part = gate_grad.shape[2]
        total = jnp.zeros(out_ref.shape, jnp.float32)
        for k in range(parts):
            columns = slice(k * part, (k + 1) * part)
            total += contract_last(gate_grad[k], gate_ref[:, columns])
            total += contract_last(up_grad[k], up_ref[:, columns])
        out_ref[...] = total.astype(out_ref.dtype)


def expert_backward(scaled, pre_gate, pre_up, gate_matrix, up_matrix, down_matrix):
    count, width = scaled.shape
    hidden = gate_matrix.shape[1]
    part, column = piece(hidden, 256), piece(width, 256)
    parts, columns = hidden // part, width // column
    early = lambda i: (0, jnp.minimum(i, parts - 1))
    late = lambda i: (jnp.maximum(i - parts, 0), 0)
    return pl.pallas_call(
        functools.partial(backward_kernel, parts),
        grid=(parts + columns,),
        in_specs=[
            pl.BlockSpec((count, width), lambda i: (0, 0)),
            pl.BlockSpec((count, part), early),
            pl.BlockSpec((count, part), early),
            pl.BlockSpec((part, width), lambda i: (jnp.minimum(i, parts - 1), 0)),
            pl.BlockSpec((column, hidden), late),
            pl.BlockSpec((column, hidden), late),
        ],
        out_specs=pl.BlockSpec((count, column), lambda i: (0, jnp.maximum(i - parts, 0))),
        out_shape=jax.ShapeDtypeStruct((count, width), jnp.bfloat16),
        scratch_shapes=[pltpu.VMEM((parts, count, part), jnp.bfloat16)] * 2,
        compiler_params=pltpu.CompilerParams(vmem_limit_bytes=24 * 2**20),
        cost_estimate=pl.CostEstimate(
            flops=6 * count * width * hidden,
            bytes_accessed=6 * width * hidden + 4 * count * width + 8 * count * hidden,
            transcendentals=count * hidden,
        ),
        name="expert_backward",
    )(scaled, pre_gate, pre_up, down_matrix, gate_matrix, up_matrix)


def after(value, *others):
    return lax.optimization_barrier((value,) + others)[0]


def swap(value):
    return lax.ppermute(value, "half", [(0, 1), (1, 0)])


def positions(routes, quads, slots):
    tokens, topk = routes.shape
    experts = 2 * quads
    flat = routes.reshape(-1)
    onehot = (flat[:, None] == jnp.arange(experts, dtype=jnp.int32)[None, :]).astype(jnp.bfloat16)
    count = flat.shape[0]
    row = lax.broadcasted_iota(jnp.int32, (count, count), 0)
    col = lax.broadcasted_iota(jnp.int32, (count, count), 1)
    earlier = jnp.dot(
        (col < row).astype(jnp.bfloat16), onehot, preferred_element_type=jnp.float32
    )
    rank = jnp.sum(earlier * onehot.astype(jnp.float32), axis=1).astype(jnp.int32)
    place = ((flat % quads) * 2 + flat // quads) * slots + rank
    return place.reshape(tokens, topk)


def select(place, slot_of):
    hit = place[:, 0][None, :] == slot_of[:, None]
    for k in range(1, TOPK):
        hit = hit | (place[:, k][None, :] == slot_of[:, None])
    return hit.astype(jnp.bfloat16)


def gate_of(place, gates, slot_of):
    total = jnp.zeros(slot_of.shape, jnp.float32)
    for k in range(TOPK):
        hit = place[:, k][None, :] == slot_of[:, None]
        total = total + jnp.sum(jnp.where(hit, gates[:, k].astype(jnp.float32)[None, :], 0.0), axis=1)
    return total


def local(layer_input, entering, fresh, routes, gate_weights, norm_gain, w_gate, w_up, w_down):
    quads = lax.axis_size("quad")
    experts = 2 * quads
    tokens, width = layer_input.shape[2], layer_input.shape[3]
    slots = max(2, min(tokens, 3 * tokens * TOPK // (2 * experts)))
    rows = experts * slots
    half_here = lax.axis_index("half")
    section_here = lax.axis_index("section")
    section_last = lax.axis_size("section") - 1
    gain = norm_gain[0]
    gate_matrix, up_matrix, down_matrix = w_gate[0, 0], w_up[0, 0], w_down[0, 0]

    def norm(t):
        xfloat = layer_input[t, 0].astype(jnp.float32)
        inverse = lax.rsqrt(jnp.mean(xfloat * xfloat, axis=1, keepdims=True) + 1e-05)
        return (xfloat * inverse * gain).astype(jnp.bfloat16), inverse

    def incoming_pack(values, place, gates):
        slot_of = jnp.arange(rows, dtype=jnp.int32)
        packed = jnp.dot(select(place, slot_of), values, preferred_element_type=jnp.float32)
        return (packed * gate_of(place, gates, slot_of)[:, None]).astype(jnp.bfloat16)

    index = jnp.arange(rows, dtype=jnp.int32)
    source_half = (index // slots) % 2
    own_row = source_half == half_here
    wanted = (index // (2 * slots) * 2 + half_here) * slots + index % slots

    def pair_select(own_place, mirror_place):
        own = select(own_place, jnp.where(own_row, wanted, -1))
        mirror = select(mirror_place, jnp.where(own_row, -1, wanted))
        return jnp.concatenate([own, mirror], axis=1)

    def pair_gate(own_place, own_gates, mirror_place, mirror_gates):
        own = gate_of(own_place, own_gates, jnp.where(own_row, wanted, -1))
        mirror = gate_of(mirror_place, mirror_gates, jnp.where(own_row, -1, wanted))
        return own + mirror

    def exchange(packed, axes):
        return lax.all_to_all(
            packed.reshape(lax.axis_size(axes), -1, width), axes, split_axis=0, concat_axis=0, tiled=True
        )

    def place_rows(chosen, values):
        return jnp.dot(chosen, values, preferred_element_type=jnp.bfloat16)

    def combine(t, incoming, returned, place, inverse):
        chosen = select(place, jnp.arange(rows, dtype=jnp.int32))
        normed_grad = lax.dot_general(
            chosen, returned, (((0,), (0,)), ((), ())), preferred_element_type=jnp.float32
        )
        xfloat = layer_input[t, 0].astype(jnp.float32)
        weighted = gain * normed_grad
        project = jnp.mean(xfloat * weighted, axis=1, keepdims=True)
        return (
            incoming.astype(jnp.float32) + inverse * weighted - xfloat * inverse**3 * project
        ).astype(jnp.bfloat16)

    place = [positions(routes[t, 0], quads, slots) for t in range(TICKS)]
    gates = [gate_weights[t, 0] for t in range(TICKS)]

    grad_mirror = swap(entering[0])
    place_mirror = swap(jnp.stack(place, axis=0))
    gates_mirror = swap(gates[0])
    normed0, inverse0 = norm(0)
    normed1, inverse1 = norm(1)
    normed0_mirror = swap(after(normed0, grad_mirror))
    normed1_mirror = swap(after(normed1, normed0_mirror))

    half_index = jnp.arange(quads * slots, dtype=jnp.int32)
    half_wanted = (half_index // slots * 2 + half_here) * slots + half_index % slots
    rows1_own = exchange(place_rows(select(place[1], half_wanted), normed1), "quad")

    pair0 = pair_select(place[0], place_mirror[0])
    scale0 = pair_gate(place[0], gates[0], place_mirror[0], gates_mirror)

    both = jnp.concatenate([entering[0], grad_mirror], axis=0)
    packed = jnp.dot(pair0, both, preferred_element_type=jnp.float32)
    packed = (packed * scale0[:, None]).astype(jnp.bfloat16)
    scaled0 = exchange(after(packed, rows1_own), "quad").reshape(rows, width)

    both = jnp.concatenate([normed0, normed0_mirror], axis=0)
    rows0 = exchange(after(place_rows(pair0, both), scaled0), "quad").reshape(rows, width)
    pre_gate0, pre_up0 = pre_activations(after(rows0, normed1_mirror), gate_matrix, up_matrix)
    computed0 = expert_backward(scaled0, pre_gate0, pre_up0, gate_matrix, up_matrix, down_matrix)
    packed1 = place_rows(select(place_mirror[1], half_wanted), normed1_mirror)
    returned0 = exchange(computed0, BOTH).reshape(rows, width)
    rows1_mirror = exchange(after(packed1, returned0), "quad")
    result0 = combine(0, entering[0], returned0, place[0], inverse0)

    length = section_last + 1
    arrived = lax.ppermute(result0, "section", [(i, i - 1) for i in range(1, length)])
    incoming = jnp.where(section_here == section_last, fresh[0], arrived)
    scaled1 = after(incoming_pack(incoming, place[1], gates[1]), rows1_mirror)
    scaled1 = exchange(scaled1, BOTH).reshape(rows, width)
    first = half_here == 0
    rows1 = jnp.stack(
        [jnp.where(first, rows1_own, rows1_mirror), jnp.where(first, rows1_mirror, rows1_own)], axis=1
    ).reshape(rows, width)
    pre_gate1, pre_up1 = pre_activations(rows1, gate_matrix, up_matrix)
    computed1 = expert_backward(scaled1, pre_gate1, pre_up1, gate_matrix, up_matrix, down_matrix)
    returned1 = exchange(computed1, BOTH).reshape(rows, width)
    result1 = combine(1, incoming, returned1, place[1], inverse1)
    return jnp.stack([result0, result1], axis=0)[:, None]


def solution(mesh):
    sections, experts = mesh.shape["section"], mesh.shape["expert"]
    split = Mesh(mesh.devices.reshape(sections, 2, experts // 2), ("section", "half", "quad"))
    expert = ("half", "quad")
    in_specs = (
        P(None, "section", expert, None),
        P("section", expert, None),
        P(None, expert, None),
        P(None, "section", expert, None),
        P(None, "section", expert, None),
        P("section", None),
        P("section", expert, None, None),
        P("section", expert, None, None),
        P("section", expert, None, None),
    )
    out_specs = P(None, "section", expert, None)
    return jax.shard_map(local, mesh=split, in_specs=in_specs, out_specs=out_specs, check_vma=False)
```

```python
import functools

import jax
import jax.numpy as jnp
from jax import lax
from jax.experimental import pallas as pl
from jax.experimental.pallas import tpu as pltpu
from jax.sharding import PartitionSpec as P

TICKS = 2
TOPK = 2
SUBLANES = 16

VMEM_WHOLE = pl.BlockSpec(memory_space=pltpu.VMEM)


def piece(size, want):
    return want if size % want == 0 else size


def contract_last(left, right):
    return lax.dot_general(
        left, right, (((1,), (1,)), ((), ())), preferred_element_type=jnp.float32
    )


def params(limit=16):
    return pltpu.CompilerParams(vmem_limit_bytes=limit * 2**20)


def aligned(slots):
    return slots % SUBLANES == 0


def slab_shapes(slabs, slots, width):
    if aligned(slots):
        return [jax.ShapeDtypeStruct((slots, width), jnp.bfloat16)] * slabs
    return [jax.ShapeDtypeStruct((slabs * slots, width), jnp.bfloat16)]


def to_slabs(outs, slabs, slots):
    if aligned(slots):
        return list(outs)
    return [outs[0][k * slots : (k + 1) * slots] for k in range(slabs)]


def from_slabs(slabs):
    if aligned(slabs[0].shape[0]):
        return list(slabs)
    return [jnp.concatenate(slabs, axis=0)]


def store_slabs(value, refs, columns):
    rows = refs[0].shape[0]
    for k, ref in enumerate(refs):
        ref[:, columns] = value[k * rows : (k + 1) * rows].astype(ref.dtype)


def gather_slabs(refs, rows_ref):
    start = 0
    for ref in refs:
        rows_ref[start : start + ref.shape[0], :] = ref[...]
        start += ref.shape[0]


def slot_hits(info_ref, first, rows, base):
    slot = lax.broadcasted_iota(jnp.int32, (rows, info_ref.shape[1]), 0) + base
    return [slot == info_ref[first + k : first + k + 1, :].astype(jnp.int32) for k in range(TOPK)]


def one_hot(hits):
    total = jnp.where(hits[0], 1.0, 0.0)
    for hit in hits[1:]:
        total = total + jnp.where(hit, 1.0, 0.0)
    return total.astype(jnp.bfloat16)


def slot_gates(hits, info_ref, first):
    total = jnp.zeros((hits[0].shape[0], 1), jnp.float32)
    for k, hit in enumerate(hits):
        gates = info_ref[first + k : first + k + 1, :]
        total = total + jnp.sum(jnp.where(hit, gates, 0.0), axis=1, keepdims=True)
    return total


def inverse_of(x_ref):
    xfloat = x_ref[...].astype(jnp.float32)
    return lax.rsqrt(jnp.mean(xfloat * xfloat, axis=1, keepdims=True) + 1e-05)


def whole(shape):
    return pl.BlockSpec(shape, lambda *_: (0,) * len(shape))


def pack_normed_kernel(rows, first, base, info_ref, x_ref, gain_ref, *outs):
    chosen = one_hot(slot_hits(info_ref, first, rows, base))
    inverse = inverse_of(x_ref)
    width = x_ref.shape[1]
    part = piece(width, 512)
    for start in range(0, width, part):
        columns = slice(start, start + part)
        normed = (x_ref[:, columns].astype(jnp.float32) * inverse * gain_ref[:, columns]).astype(
            jnp.bfloat16
        )
        store_slabs(jnp.dot(chosen, normed, preferred_element_type=jnp.float32), outs, columns)


def pack_scaled_kernel(rows, first, base, info_ref, values_ref, *outs):
    hits = slot_hits(info_ref, first, rows, base)
    chosen = one_hot(hits)
    gates = slot_gates(hits, info_ref, 2 * TOPK + first)
    width = values_ref.shape[1]
    part = piece(width, 512)
    for start in range(0, width, part):
        columns = slice(start, start + part)
        packed = jnp.dot(chosen, values_ref[:, columns], preferred_element_type=jnp.float32)
        store_slabs(packed * gates, outs, columns)


def call_pack(kernel, slabs, slots, first, base, arrays):
    width = arrays[1].shape[1]
    rows = slabs * slots
    outs = pl.pallas_call(
        functools.partial(kernel, rows, first, base),
        in_specs=[whole(a.shape) for a in arrays],
        out_specs=[whole(s.shape) for s in slab_shapes(slabs, slots, width)],
        out_shape=slab_shapes(slabs, slots, width),
        grid=(1,),
        compiler_params=params(),
        cost_estimate=pl.CostEstimate(
            flops=2 * rows * arrays[1].shape[0] * width,
            bytes_accessed=2 * rows * width + 2 * arrays[1].size,
            transcendentals=0,
        ),
    )(*arrays)
    return to_slabs(outs, slabs, slots)


def resident(value):
    return pltpu.with_memory_space_constraint(value, pltpu.VMEM)


def pre_kernel(part, *refs):
    *slabs, gate_ref, up_ref, pre_gate_ref, pre_up_ref, rows_ref = refs
    gather_slabs(slabs, rows_ref)
    for start in range(0, gate_ref.shape[1], part):
        columns = slice(start, start + part)
        rows = rows_ref[...]
        pre_gate_ref[:, columns] = jnp.dot(rows, gate_ref[:, columns], preferred_element_type=jnp.float32)
        pre_up_ref[:, columns] = jnp.dot(rows, up_ref[:, columns], preferred_element_type=jnp.float32)


def pre_activations(slabs, gate_matrix, up_matrix):
    slabs = from_slabs(slabs)
    count, width = sum(s.shape[0] for s in slabs), slabs[0].shape[1]
    hidden = gate_matrix.shape[1]
    return pl.pallas_call(
        functools.partial(pre_kernel, piece(hidden, 256)),
        in_specs=[VMEM_WHOLE] * (len(slabs) + 2),
        out_specs=[VMEM_WHOLE] * 2,
        out_shape=[jax.ShapeDtypeStruct((count, hidden), jnp.float32)] * 2,
        scratch_shapes=[pltpu.VMEM((count, width), jnp.bfloat16)],
        compiler_params=params(16),
        cost_estimate=pl.CostEstimate(
            flops=4 * count * width * hidden,
            bytes_accessed=4 * width * hidden + 2 * count * width + 8 * count * hidden,
            transcendentals=0,
        ),
        name="pre_activations",
    )(*slabs, resident(gate_matrix), resident(up_matrix))


def backward_kernel(part, column, count_in, *refs):
    slabs, refs = refs[:count_in], refs[count_in:]
    pre_gate_ref, pre_up_ref, down_ref, gate_ref, up_ref, *outs = refs
    *outs, rows_ref, gate_grad, up_grad = outs
    gather_slabs(slabs, rows_ref)
    for start in range(0, gate_ref.shape[1], part):
        columns = slice(start, start + part)
        hidden_grad = contract_last(rows_ref[...], down_ref[columns, :])
        pre_gate = pre_gate_ref[:, columns]
        sigmoid = 1.0 / (1.0 + jnp.exp(-pre_gate))
        both = hidden_grad * sigmoid
        gate_grad[:, columns] = (
            both * pre_up_ref[:, columns] * (1.0 + pre_gate * (1.0 - sigmoid))
        ).astype(jnp.bfloat16)
        up_grad[:, columns] = (both * pre_gate).astype(jnp.bfloat16)
    for start in range(0, gate_ref.shape[0], column):
        chosen = slice(start, start + column)
        total = contract_last(gate_grad[...], gate_ref[chosen, :]) + contract_last(
            up_grad[...], up_ref[chosen, :]
        )
        store_slabs(total, outs, chosen)


def expert_backward(slabs, slots, pre_gate, pre_up, gate_matrix, up_matrix, down_matrix):
    number = len(slabs)
    slabs = from_slabs(slabs)
    count, width = sum(s.shape[0] for s in slabs), slabs[0].shape[1]
    hidden = gate_matrix.shape[1]
    shapes = slab_shapes(number, slots, width)
    outs = pl.pallas_call(
        functools.partial(backward_kernel, piece(hidden, 256), piece(width, 256), len(slabs)),
        in_specs=[VMEM_WHOLE] * (len(slabs) + 5),
        out_specs=[VMEM_WHOLE] * len(shapes),
        out_shape=shapes,
        scratch_shapes=[pltpu.VMEM((count, width), jnp.bfloat16)]
        + [pltpu.VMEM((count, hidden), jnp.bfloat16)] * 2,
        compiler_params=params(16),
        cost_estimate=pl.CostEstimate(
            flops=6 * count * width * hidden,
            bytes_accessed=6 * width * hidden + 4 * count * width + 8 * count * hidden,
            transcendentals=count * hidden,
        ),
        name="expert_backward",
    )(*slabs, pre_gate, pre_up, resident(down_matrix), resident(gate_matrix), resident(up_matrix))
    return to_slabs(outs, number, slots)


def combined(slabs, info_ref, first, x_ref, incoming_of, gain_ref, rows_ref, weighted_ref, put):
    gather_slabs(slabs, rows_ref)
    rows, width = rows_ref.shape
    chosen = one_hot(slot_hits(info_ref, first, rows, 0))
    inverse = inverse_of(x_ref)
    part = piece(width, 512)
    project = None
    for start in range(0, width, part):
        columns = slice(start, start + part)
        normed_grad = lax.dot_general(
            chosen, rows_ref[:, columns], (((0,), (0,)), ((), ())), preferred_element_type=jnp.float32
        )
        weighted = gain_ref[:, columns] * normed_grad
        weighted_ref[:, columns] = weighted
        term = jnp.sum(x_ref[:, columns].astype(jnp.float32) * weighted, axis=1, keepdims=True)
        project = term if project is None else project + term
    factor = inverse * inverse * inverse * (project / width)
    for start in range(0, width, part):
        columns = slice(start, start + part)
        put(
            columns,
            (
                incoming_of(columns).astype(jnp.float32)
                + inverse * weighted_ref[:, columns]
                - x_ref[:, columns].astype(jnp.float32) * factor
            ).astype(jnp.bfloat16),
        )


def relay_kernel(count_in, *refs):
    slabs, refs = refs[:count_in], refs[count_in:]
    flag_ref, info_ref, next_ref, x_ref, incoming_ref, fresh_ref, gain_ref, result_ref, *outs = refs
    *outs, rows_ref, weighted_ref = outs
    rows = rows_ref.shape[0]
    hits = slot_hits(next_ref, TOPK, rows, 0)
    chosen = one_hot(hits)
    gates = slot_gates(hits, next_ref, 3 * TOPK)
    takes_fresh = flag_ref[0] == 0

    def put(columns, value):
        result_ref[:, columns] = value
        passed = jnp.where(takes_fresh, fresh_ref[:, columns], value)
        store_slabs(jnp.dot(chosen, passed, preferred_element_type=jnp.float32) * gates, outs, columns)

    combined(slabs, info_ref, 0, x_ref, lambda c: incoming_ref[:, c], gain_ref, rows_ref, weighted_ref, put)


def final_kernel(count_in, *refs):
    slabs, refs = refs[:count_in], refs[count_in:]
    flag_ref, info_ref, x_ref, arrived_ref, fresh_ref, gain_ref, result_ref, out_ref = refs[:8]
    rows_ref, weighted_ref = refs[8:]
    out_ref[0] = result_ref[...]
    takes_fresh = flag_ref[1] == 0

    def put(columns, value):
        out_ref[1, :, columns] = value

    def incoming_of(columns):
        return jnp.where(takes_fresh, fresh_ref[:, columns], arrived_ref[:, columns])

    combined(slabs, info_ref, TOPK, x_ref, incoming_of, gain_ref, rows_ref, weighted_ref, put)


def call_combine(kernel, slabs, arrays, shapes):
    slabs = from_slabs(slabs)
    count, width = sum(s.shape[0] for s in slabs), slabs[0].shape[1]
    tokens = arrays[-1].shape[0]
    specs = [whole(s.shape) for s in slabs] + [pl.BlockSpec(memory_space=pltpu.SMEM)]
    return pl.pallas_call(
        functools.partial(kernel, len(slabs)),
        in_specs=specs + [whole(a.shape) for a in arrays[1:]],
        out_specs=[whole(s.shape) for s in shapes],
        out_shape=shapes,
        grid=(1,),
        scratch_shapes=[
            pltpu.VMEM((count, width), jnp.bfloat16),
            pltpu.VMEM((shapes[0].shape[-2], width), jnp.float32),
        ],
        compiler_params=params(),
        cost_estimate=pl.CostEstimate(
            flops=4 * count * tokens * width, bytes_accessed=4 * count * width, transcendentals=0
        ),
    )(*slabs, *arrays)


def local(layer_input, entering, fresh, routes, gate_weights, norm_gain, w_gate, w_up, w_down):
    experts = lax.axis_size("expert")
    sections = lax.axis_size("section")
    tokens, width = layer_input.shape[2], layer_input.shape[3]
    slots = max(2, min(tokens, 3 * tokens * TOPK // (2 * experts)))
    half = experts // 2
    here = lax.axis_index("expert")
    section_here = lax.axis_index("section")
    gate_matrix, up_matrix, down_matrix = w_gate[0, 0], w_up[0, 0], w_down[0, 0]
    layer_rows = [layer_input[t, 0] for t in range(TICKS)]
    token_rows = jax.ShapeDtypeStruct((tokens, width), jnp.bfloat16)

    def across(value, k):
        return lax.ppermute(value, "expert", [(i, i ^ k) for i in range(experts)])

    def deal(slabs):
        return [slabs[0]] + [across(slabs[k], k) for k in range(1, len(slabs))]

    def previous(value, k):
        pairs = [
            (s * experts + i, (s - 1) % sections * experts + (i ^ k))
            for s in range(sections)
            for i in range(experts)
        ]
        return lax.ppermute(value, ("section", "expert"), pairs)

    grad_mirror = across(entering[0], half)

    chosen = routes[:, 0].transpose(0, 2, 1)
    expert_ids = jnp.arange(experts, dtype=jnp.int32)
    onehot = chosen[:, :, None, :] == expert_ids[None, None, :, None]
    named = jnp.sum(onehot.astype(jnp.float32), axis=1).astype(jnp.bfloat16)
    order = jnp.arange(tokens, dtype=jnp.int32)
    before = (order[:, None] < order[None, :]).astype(jnp.bfloat16)
    counted = lax.dot_general(
        named, before, (((2,), (0,)), ((), ())), preferred_element_type=jnp.float32
    )
    rank = jnp.sum(jnp.where(onehot, counted[:, None], 0.0), axis=2)
    place = (chosen ^ here).astype(jnp.float32) * slots + rank
    gates = gate_weights[:, 0].transpose(0, 2, 1).astype(jnp.float32)
    info = jnp.concatenate([place, gates], axis=0).reshape(2 * TICKS * TOPK, tokens)
    info_mirror = across(info, half)
    info_next = lax.ppermute(info, "section", [(s, (s + 1) % sections) for s in range(sections)])
    x0_mirror = across(layer_rows[0], half)

    def normed(t, values, given, base):
        return call_pack(pack_normed_kernel, half, slots, TOPK * t, base * slots, [given, values, norm_gain])

    def scaled(values, given, base):
        return call_pack(pack_scaled_kernel, half, slots, 0, base * slots, [given, values])

    scaled0 = deal(scaled(entering[0], info, 0))
    rows0 = deal(normed(0, layer_rows[0], info, 0))
    scaled0 += deal(scaled(grad_mirror, info_mirror, half))
    rows0 += deal(normed(0, x0_mirror, info_mirror, half))
    x1_mirror = across(layer_rows[1], half)

    pre_gate0, pre_up0 = pre_activations(rows0, gate_matrix, up_matrix)
    computed0 = expert_backward(scaled0, slots, pre_gate0, pre_up0, gate_matrix, up_matrix, down_matrix)
    returned0 = deal(computed0)
    rows1 = deal(normed(1, layer_rows[1], info, 0))
    rows1 += deal(normed(1, x1_mirror, info_mirror, half))

    flags = jnp.stack([section_here, sections - 1 - section_here]).astype(jnp.int32)
    relayed = call_combine(
        relay_kernel,
        returned0,
        [flags, info, info_next, layer_rows[0], entering[0], fresh[0], norm_gain],
        [token_rows] + slab_shapes(experts, slots, width),
    )
    result0 = relayed[0]
    outgoing = to_slabs(relayed[1:], experts, slots)
    scaled1 = [previous(outgoing[k], k) for k in range(experts)]
    arrived = previous(result0, 0)
    pre_gate1, pre_up1 = pre_activations(rows1, gate_matrix, up_matrix)
    computed1 = expert_backward(scaled1, slots, pre_gate1, pre_up1, gate_matrix, up_matrix, down_matrix)
    returned1 = deal(computed1)
    (out,) = call_combine(
        final_kernel,
        returned1,
        [flags, info, layer_rows[1], arrived, fresh[0], norm_gain, result0],
        [jax.ShapeDtypeStruct((TICKS, tokens, width), jnp.bfloat16)],
    )
    return out[:, None]


def solution(mesh):
    in_specs = (
        P(None, "section", "expert", None),
        P("section", "expert", None),
        P(None, "expert", None),
        P(None, "section", "expert", None),
        P(None, "section", "expert", None),
        P("section", None),
        P("section", "expert", None, None),
        P("section", "expert", None, None),
        P("section", "expert", None, None),
    )
    out_specs = P(None, "section", "expert", None)

    return jax.shard_map(local, mesh=mesh, in_specs=in_specs, out_specs=out_specs, check_vma=False)
```

```python
import functools

import jax
import jax.numpy as jnp
from jax import lax
from jax.experimental import pallas as pl
from jax.experimental.pallas import tpu as pltpu
from jax.sharding import PartitionSpec as P

TICKS = 2
TOPK = 2
SUBLANES = 16

VMEM_WHOLE = pl.BlockSpec(memory_space=pltpu.VMEM)


def piece(size, want):
    return want if size % want == 0 else size


def contract_last(left, right):
    return lax.dot_general(
        left, right, (((1,), (1,)), ((), ())), preferred_element_type=jnp.float32
    )


def params(limit=16):
    return pltpu.CompilerParams(vmem_limit_bytes=limit * 2**20)


def aligned(slots):
    return slots % SUBLANES == 0


def slab_shapes(slabs, slots, width):
    if aligned(slots):
        return [jax.ShapeDtypeStruct((slots, width), jnp.bfloat16)] * slabs
    return [jax.ShapeDtypeStruct((slabs * slots, width), jnp.bfloat16)]


def to_slabs(outs, slabs, slots):
    if aligned(slots):
        return list(outs)
    return [outs[0][k * slots : (k + 1) * slots] for k in range(slabs)]


def from_slabs(slabs):
    if aligned(slabs[0].shape[0]):
        return list(slabs)
    return [jnp.concatenate(slabs, axis=0)]


def store_slabs(value, refs, columns):
    rows = refs[0].shape[0]
    for k, ref in enumerate(refs):
        ref[:, columns] = value[k * rows : (k + 1) * rows].astype(ref.dtype)


def gather_slabs(refs, rows_ref):
    start = 0
    for ref in refs:
        rows_ref[start : start + ref.shape[0], :] = ref[...]
        start += ref.shape[0]


def slot_hits(info_ref, first, rows, base):
    slot = lax.broadcasted_iota(jnp.int32, (rows, info_ref.shape[1]), 0) + base
    return [slot == info_ref[first + k : first + k + 1, :].astype(jnp.int32) for k in range(TOPK)]


def one_hot(hits):
    total = jnp.where(hits[0], 1.0, 0.0)
    for hit in hits[1:]:
        total = total + jnp.where(hit, 1.0, 0.0)
    return total.astype(jnp.bfloat16)


def slot_gates(hits, info_ref, first):
    total = jnp.zeros((hits[0].shape[0], 1), jnp.float32)
    for k, hit in enumerate(hits):
        gates = info_ref[first + k : first + k + 1, :]
        total = total + jnp.sum(jnp.where(hit, gates, 0.0), axis=1, keepdims=True)
    return total


def inverse_of(x_ref):
    xfloat = x_ref[...].astype(jnp.float32)
    return lax.rsqrt(jnp.mean(xfloat * xfloat, axis=1, keepdims=True) + 1e-05)


def whole(shape):
    return pl.BlockSpec(shape, lambda *_: (0,) * len(shape))


def pack_normed_kernel(rows, first, base, info_ref, x_ref, gain_ref, *outs):
    chosen = one_hot(slot_hits(info_ref, first, rows, base))
    inverse = inverse_of(x_ref)
    width = x_ref.shape[1]
    part = piece(width, 512)
    for start in range(0, width, part):
        columns = slice(start, start + part)
        normed = (x_ref[:, columns].astype(jnp.float32) * inverse * gain_ref[:, columns]).astype(
            jnp.bfloat16
        )
        store_slabs(jnp.dot(chosen, normed, preferred_element_type=jnp.float32), outs, columns)


def pack_scaled_kernel(rows, first, base, info_ref, values_ref, *outs):
    hits = slot_hits(info_ref, first, rows, base)
    chosen = one_hot(hits)
    gates = slot_gates(hits, info_ref, 2 * TOPK + first)
    width = values_ref.shape[1]
    part = piece(width, 512)
    for start in range(0, width, part):
        columns = slice(start, start + part)
        packed = jnp.dot(chosen, values_ref[:, columns], preferred_element_type=jnp.float32)
        store_slabs(packed * gates, outs, columns)


def call_pack(kernel, slabs, slots, first, base, arrays):
    width = arrays[1].shape[1]
    rows = slabs * slots
    outs = pl.pallas_call(
        functools.partial(kernel, rows, first, base),
        in_specs=[whole(a.shape) for a in arrays],
        out_specs=[whole(s.shape) for s in slab_shapes(slabs, slots, width)],
        out_shape=slab_shapes(slabs, slots, width),
        grid=(1,),
        compiler_params=params(),
        cost_estimate=pl.CostEstimate(
            flops=2 * rows * arrays[1].shape[0] * width,
            bytes_accessed=2 * rows * width + 2 * arrays[1].size,
            transcendentals=0,
        ),
    )(*arrays)
    return to_slabs(outs, slabs, slots)


def resident(value):
    return pltpu.with_memory_space_constraint(value, pltpu.VMEM)


def pre_kernel(part, *refs):
    *slabs, gate_ref, up_ref, pre_gate_ref, pre_up_ref, rows_ref = refs
    gather_slabs(slabs, rows_ref)
    for start in range(0, gate_ref.shape[1], part):
        columns = slice(start, start + part)
        rows = rows_ref[...]
        pre_gate_ref[:, columns] = jnp.dot(rows, gate_ref[:, columns], preferred_element_type=jnp.float32)
        pre_up_ref[:, columns] = jnp.dot(rows, up_ref[:, columns], preferred_element_type=jnp.float32)


def pre_activations(slabs, gate_matrix, up_matrix):
    slabs = from_slabs(slabs)
    count, width = sum(s.shape[0] for s in slabs), slabs[0].shape[1]
    hidden = gate_matrix.shape[1]
    return pl.pallas_call(
        functools.partial(pre_kernel, piece(hidden, 256)),
        in_specs=[VMEM_WHOLE] * (len(slabs) + 2),
        out_specs=[VMEM_WHOLE] * 2,
        out_shape=[jax.ShapeDtypeStruct((count, hidden), jnp.float32)] * 2,
        scratch_shapes=[pltpu.VMEM((count, width), jnp.bfloat16)],
        compiler_params=params(16),
        cost_estimate=pl.CostEstimate(
            flops=4 * count * width * hidden,
            bytes_accessed=4 * width * hidden + 2 * count * width + 8 * count * hidden,
            transcendentals=0,
        ),
        name="pre_activations",
    )(*slabs, resident(gate_matrix), resident(up_matrix))


def hidden_kernel(part, *refs):
    *slabs, down_ref, hidden_ref, rows_ref = refs
    gather_slabs(slabs, rows_ref)
    for start in range(0, down_ref.shape[0], part):
        columns = slice(start, start + part)
        hidden_ref[:, columns] = contract_last(rows_ref[...], down_ref[columns, :])


def hidden_gradient(slabs, down_matrix):
    slabs = from_slabs(slabs)
    count, width = sum(s.shape[0] for s in slabs), slabs[0].shape[1]
    hidden = down_matrix.shape[0]
    return pl.pallas_call(
        functools.partial(hidden_kernel, piece(hidden, 256)),
        in_specs=[VMEM_WHOLE] * (len(slabs) + 1),
        out_specs=VMEM_WHOLE,
        out_shape=jax.ShapeDtypeStruct((count, hidden), jnp.float32),
        scratch_shapes=[pltpu.VMEM((count, width), jnp.bfloat16)],
        compiler_params=params(16),
        cost_estimate=pl.CostEstimate(
            flops=2 * count * width * hidden,
            bytes_accessed=2 * width * hidden + 2 * count * width + 4 * count * hidden,
            transcendentals=0,
        ),
        name="hidden_gradient",
    )(*slabs, resident(down_matrix))


def store_grads(pre_gate, pre_up, hidden_grad, gate_grad, up_grad, columns):
    sigmoid = 1.0 / (1.0 + jnp.exp(-pre_gate))
    both = hidden_grad * sigmoid
    gate_grad[:, columns] = (both * pre_up * (1.0 + pre_gate * (1.0 - sigmoid))).astype(jnp.bfloat16)
    up_grad[:, columns] = (both * pre_gate).astype(jnp.bfloat16)


def store_rows(gate_grad, up_grad, gate_ref, up_ref, outs, column):
    for start in range(0, gate_ref.shape[0], column):
        chosen = slice(start, start + column)
        total = contract_last(gate_grad[...], gate_ref[chosen, :]) + contract_last(
            up_grad[...], up_ref[chosen, :]
        )
        store_slabs(total, outs, chosen)


def gradient_last_kernel(part, column, count_in, *refs):
    slabs, refs = refs[:count_in], refs[count_in:]
    pre_gate_ref, pre_up_ref, down_ref, gate_ref, up_ref, *outs = refs
    *outs, rows_ref, gate_grad, up_grad = outs
    gather_slabs(slabs, rows_ref)
    for start in range(0, gate_ref.shape[1], part):
        columns = slice(start, start + part)
        hidden_grad = contract_last(rows_ref[...], down_ref[columns, :])
        store_grads(
            pre_gate_ref[:, columns], pre_up_ref[:, columns], hidden_grad, gate_grad, up_grad, columns
        )
    store_rows(gate_grad, up_grad, gate_ref, up_ref, outs, column)


def normed_last_kernel(part, column, count_in, *refs):
    slabs, refs = refs[:count_in], refs[count_in:]
    pre_gate_ref, pre_up_ref, hidden_ref, gate_ref, up_ref, *outs = refs
    *outs, rows_ref, gate_grad, up_grad = outs
    gather_slabs(slabs, rows_ref)
    for start in range(0, gate_ref.shape[1], part):
        columns = slice(start, start + part)
        far_gate = jnp.dot(rows_ref[...], gate_ref[:, columns], preferred_element_type=jnp.float32)
        far_up = jnp.dot(rows_ref[...], up_ref[:, columns], preferred_element_type=jnp.float32)
        pre_gate = jnp.concatenate([pre_gate_ref[:, columns], far_gate], axis=0)
        pre_up = jnp.concatenate([pre_up_ref[:, columns], far_up], axis=0)
        store_grads(pre_gate, pre_up, hidden_ref[:, columns], gate_grad, up_grad, columns)
    store_rows(gate_grad, up_grad, gate_ref, up_ref, outs, column)


def call_backward(kernel, slabs, number, slots, given, matrices):
    slabs = from_slabs(slabs)
    count, width = number * slots, slabs[0].shape[1]
    gathered = sum(s.shape[0] for s in slabs)
    hidden = matrices[-1].shape[1]
    shapes = slab_shapes(number, slots, width)
    outs = pl.pallas_call(
        functools.partial(kernel, piece(hidden, 256), piece(width, 256), len(slabs)),
        in_specs=[VMEM_WHOLE] * (len(slabs) + len(given) + len(matrices)),
        out_specs=[VMEM_WHOLE] * len(shapes),
        out_shape=shapes,
        scratch_shapes=[pltpu.VMEM((gathered, width), jnp.bfloat16)]
        + [pltpu.VMEM((count, hidden), jnp.bfloat16)] * 2,
        compiler_params=params(16),
        cost_estimate=pl.CostEstimate(
            flops=6 * count * width * hidden,
            bytes_accessed=6 * width * hidden + 4 * count * width + 8 * count * hidden,
            transcendentals=count * hidden,
        ),
        name="expert_backward",
    )(*slabs, *given, *[resident(m) for m in matrices])
    return to_slabs(outs, number, slots)


def combined(slabs, info_ref, first, x_ref, incoming_of, gain_ref, rows_ref, weighted_ref, put):
    gather_slabs(slabs, rows_ref)
    rows, width = rows_ref.shape
    chosen = one_hot(slot_hits(info_ref, first, rows, 0))
    inverse = inverse_of(x_ref)
    part = piece(width, 512)
    project = None
    for start in range(0, width, part):
        columns = slice(start, start + part)
        normed_grad = lax.dot_general(
            chosen, rows_ref[:, columns], (((0,), (0,)), ((), ())), preferred_element_type=jnp.float32
        )
        weighted = gain_ref[:, columns] * normed_grad
        weighted_ref[:, columns] = weighted
        term = jnp.sum(x_ref[:, columns].astype(jnp.float32) * weighted, axis=1, keepdims=True)
        project = term if project is None else project + term
    factor = inverse * inverse * inverse * (project / width)
    for start in range(0, width, part):
        columns = slice(start, start + part)
        put(
            columns,
            (
                incoming_of(columns).astype(jnp.float32)
                + inverse * weighted_ref[:, columns]
                - x_ref[:, columns].astype(jnp.float32) * factor
            ).astype(jnp.bfloat16),
        )


def relay_kernel(count_in, *refs):
    slabs, refs = refs[:count_in], refs[count_in:]
    flag_ref, info_ref, next_ref, x_ref, incoming_ref, fresh_ref, gain_ref, result_ref, *outs = refs
    *outs, rows_ref, weighted_ref = outs
    rows = rows_ref.shape[0]
    hits = slot_hits(next_ref, TOPK, rows, 0)
    chosen = one_hot(hits)
    gates = slot_gates(hits, next_ref, 3 * TOPK)
    takes_fresh = flag_ref[0] == 0

    def put(columns, value):
        result_ref[:, columns] = value
        passed = jnp.where(takes_fresh, fresh_ref[:, columns], value)
        store_slabs(jnp.dot(chosen, passed, preferred_element_type=jnp.float32) * gates, outs, columns)

    combined(slabs, info_ref, 0, x_ref, lambda c: incoming_ref[:, c], gain_ref, rows_ref, weighted_ref, put)


def final_kernel(count_in, *refs):
    slabs, refs = refs[:count_in], refs[count_in:]
    flag_ref, info_ref, x_ref, arrived_ref, fresh_ref, gain_ref, result_ref, out_ref = refs[:8]
    rows_ref, weighted_ref = refs[8:]
    out_ref[0] = result_ref[...]
    takes_fresh = flag_ref[1] == 0

    def put(columns, value):
        out_ref[1, :, columns] = value

    def incoming_of(columns):
        return jnp.where(takes_fresh, fresh_ref[:, columns], arrived_ref[:, columns])

    combined(slabs, info_ref, TOPK, x_ref, incoming_of, gain_ref, rows_ref, weighted_ref, put)


def call_combine(kernel, slabs, arrays, shapes):
    slabs = from_slabs(slabs)
    count, width = sum(s.shape[0] for s in slabs), slabs[0].shape[1]
    tokens = arrays[-1].shape[0]
    specs = [whole(s.shape) for s in slabs] + [pl.BlockSpec(memory_space=pltpu.SMEM)]
    return pl.pallas_call(
        functools.partial(kernel, len(slabs)),
        in_specs=specs + [whole(a.shape) for a in arrays[1:]],
        out_specs=[whole(s.shape) for s in shapes],
        out_shape=shapes,
        grid=(1,),
        scratch_shapes=[
            pltpu.VMEM((count, width), jnp.bfloat16),
            pltpu.VMEM((shapes[0].shape[-2], width), jnp.float32),
        ],
        compiler_params=params(),
        cost_estimate=pl.CostEstimate(
            flops=4 * count * tokens * width, bytes_accessed=4 * count * width, transcendentals=0
        ),
    )(*slabs, *arrays)


def local(layer_input, entering, fresh, routes, gate_weights, norm_gain, w_gate, w_up, w_down):
    experts = lax.axis_size("expert")
    sections = lax.axis_size("section")
    tokens, width = layer_input.shape[2], layer_input.shape[3]
    slots = max(2, min(tokens, 3 * tokens * TOPK // (2 * experts)))
    half = experts // 2
    here = lax.axis_index("expert")
    section_here = lax.axis_index("section")
    gate_matrix, up_matrix, down_matrix = w_gate[0, 0], w_up[0, 0], w_down[0, 0]
    layer_rows = [layer_input[t, 0] for t in range(TICKS)]
    token_rows = jax.ShapeDtypeStruct((tokens, width), jnp.bfloat16)

    def across(value, k):
        return lax.ppermute(value, "expert", [(i, i ^ k) for i in range(experts)])

    def deal(slabs):
        return [slabs[0]] + [across(slabs[k], k) for k in range(1, len(slabs))]

    def previous(value, k):
        pairs = [
            (s * experts + i, (s - 1) % sections * experts + (i ^ k))
            for s in range(sections)
            for i in range(experts)
        ]
        return lax.ppermute(value, ("section", "expert"), pairs)

    grad_mirror = across(entering[0], half)

    chosen = routes[:, 0].transpose(0, 2, 1)
    expert_ids = jnp.arange(experts, dtype=jnp.int32)
    onehot = chosen[:, :, None, :] == expert_ids[None, None, :, None]
    named = jnp.sum(onehot.astype(jnp.float32), axis=1).astype(jnp.bfloat16)
    order = jnp.arange(tokens, dtype=jnp.int32)
    before = (order[:, None] < order[None, :]).astype(jnp.bfloat16)
    counted = lax.dot_general(
        named, before, (((2,), (0,)), ((), ())), preferred_element_type=jnp.float32
    )
    rank = jnp.sum(jnp.where(onehot, counted[:, None], 0.0), axis=2)
    place = (chosen ^ here).astype(jnp.float32) * slots + rank
    gates = gate_weights[:, 0].transpose(0, 2, 1).astype(jnp.float32)
    info = jnp.concatenate([place, gates], axis=0).reshape(2 * TICKS * TOPK, tokens)
    info_mirror = across(info, half)
    info_next = lax.ppermute(info, "section", [(s, (s + 1) % sections) for s in range(sections)])
    x0_mirror = across(layer_rows[0], half)

    def normed(t, values, given, base):
        return call_pack(pack_normed_kernel, half, slots, TOPK * t, base * slots, [given, values, norm_gain])

    def scaled(values, given, base):
        return call_pack(pack_scaled_kernel, half, slots, 0, base * slots, [given, values])

    scaled0 = deal(scaled(entering[0], info, 0))
    rows0 = deal(normed(0, layer_rows[0], info, 0))
    scaled0 += deal(scaled(grad_mirror, info_mirror, half))
    rows0 += deal(normed(0, x0_mirror, info_mirror, half))
    x1_mirror = across(layer_rows[1], half)

    def deal_all(slabs):
        near = deal(slabs[:half])
        return near + [across(slabs[k], k) for k in range(half, experts)]

    given = [*pre_activations(rows0[:half], gate_matrix, up_matrix)]
    given += [hidden_gradient(scaled0, down_matrix)]
    computed0 = call_backward(
        normed_last_kernel, rows0[half:], experts, slots, given, [gate_matrix, up_matrix]
    )
    returned0 = deal_all(computed0)
    rows1 = deal(normed(1, layer_rows[1], info, 0))
    rows1 += deal(normed(1, x1_mirror, info_mirror, half))

    flags = jnp.stack([section_here, sections - 1 - section_here]).astype(jnp.int32)
    relayed = call_combine(
        relay_kernel,
        returned0,
        [flags, info, info_next, layer_rows[0], entering[0], fresh[0], norm_gain],
        [token_rows] + slab_shapes(experts, slots, width),
    )
    result0 = relayed[0]
    outgoing = to_slabs(relayed[1:], experts, slots)
    scaled1 = [previous(outgoing[k], k) for k in range(half)]
    scaled1 += [previous(outgoing[k], k) for k in range(half, experts)]
    arrived = previous(result0, 0)
    given = [*pre_activations(rows1, gate_matrix, up_matrix)]
    computed1 = call_backward(
        gradient_last_kernel, scaled1, experts, slots, given, [down_matrix, gate_matrix, up_matrix]
    )
    returned1 = deal_all(computed1)
    (out,) = call_combine(
        final_kernel,
        returned1,
        [flags, info, layer_rows[1], arrived, fresh[0], norm_gain, result0],
        [jax.ShapeDtypeStruct((TICKS, tokens, width), jnp.bfloat16)],
    )
    return out[:, None]


def solution(mesh):
    in_specs = (
        P(None, "section", "expert", None),
        P("section", "expert", None),
        P(None, "expert", None),
        P(None, "section", "expert", None),
        P(None, "section", "expert", None),
        P("section", None),
        P("section", "expert", None, None),
        P("section", "expert", None, None),
        P("section", "expert", None, None),
    )
    out_specs = P(None, "section", "expert", None)

    return jax.shard_map(local, mesh=mesh, in_specs=in_specs, out_specs=out_specs, check_vma=False)
```

```python
import functools

import jax
import jax.numpy as jnp
from jax import lax
from jax.experimental import pallas as pl
from jax.experimental.pallas import tpu as pltpu
from jax.sharding import PartitionSpec as P

TICKS = 2
TOPK = 2
SUBLANES = 16

VMEM_WHOLE = pl.BlockSpec(memory_space=pltpu.VMEM)


def piece(size, want):
    return want if size % want == 0 else size


def contract_last(left, right):
    return lax.dot_general(
        left, right, (((1,), (1,)), ((), ())), preferred_element_type=jnp.float32
    )


def params(limit=16):
    return pltpu.CompilerParams(vmem_limit_bytes=limit * 2**20)


def aligned(slots):
    return slots % SUBLANES == 0


def slab_shapes(slabs, slots, width):
    if aligned(slots):
        return [jax.ShapeDtypeStruct((slots, width), jnp.bfloat16)] * slabs
    return [jax.ShapeDtypeStruct((slabs * slots, width), jnp.bfloat16)]


def to_slabs(outs, slabs, slots):
    if aligned(slots):
        return list(outs)
    return [outs[0][k * slots : (k + 1) * slots] for k in range(slabs)]


def from_slabs(slabs):
    if aligned(slabs[0].shape[0]):
        return list(slabs)
    return [jnp.concatenate(slabs, axis=0)]


def store_slabs(value, refs, columns):
    rows = refs[0].shape[0]
    for k, ref in enumerate(refs):
        ref[:, columns] = value[k * rows : (k + 1) * rows].astype(ref.dtype)


def gather_slabs(refs, rows_ref):
    start = 0
    for ref in refs:
        rows_ref[start : start + ref.shape[0], :] = ref[...]
        start += ref.shape[0]


def slot_hits(info_ref, first, rows, base):
    slot = lax.broadcasted_iota(jnp.int32, (rows, info_ref.shape[1]), 0) + base
    return [slot == info_ref[first + k : first + k + 1, :].astype(jnp.int32) for k in range(TOPK)]


def one_hot(hits):
    total = jnp.where(hits[0], 1.0, 0.0)
    for hit in hits[1:]:
        total = total + jnp.where(hit, 1.0, 0.0)
    return total.astype(jnp.bfloat16)


def slot_gates(hits, info_ref, first):
    total = jnp.zeros((hits[0].shape[0], 1), jnp.float32)
    for k, hit in enumerate(hits):
        gates = info_ref[first + k : first + k + 1, :]
        total = total + jnp.sum(jnp.where(hit, gates, 0.0), axis=1, keepdims=True)
    return total


def inverse_of(x_ref):
    xfloat = x_ref[...].astype(jnp.float32)
    return lax.rsqrt(jnp.mean(xfloat * xfloat, axis=1, keepdims=True) + 1e-05)


def whole(shape):
    return pl.BlockSpec(shape, lambda *_: (0,) * len(shape))


def pack_normed_kernel(rows, first, base, info_ref, x_ref, gain_ref, *outs):
    chosen = one_hot(slot_hits(info_ref, first, rows, base))
    inverse = inverse_of(x_ref)
    width = x_ref.shape[1]
    part = piece(width, 512)
    for start in range(0, width, part):
        columns = slice(start, start + part)
        normed = (x_ref[:, columns].astype(jnp.float32) * inverse * gain_ref[:, columns]).astype(
            jnp.bfloat16
        )
        store_slabs(jnp.dot(chosen, normed, preferred_element_type=jnp.float32), outs, columns)


def pack_scaled_kernel(rows, first, base, info_ref, values_ref, *outs):
    hits = slot_hits(info_ref, first, rows, base)
    chosen = one_hot(hits)
    gates = slot_gates(hits, info_ref, 2 * TOPK + first)
    width = values_ref.shape[1]
    part = piece(width, 512)
    for start in range(0, width, part):
        columns = slice(start, start + part)
        packed = jnp.dot(chosen, values_ref[:, columns], preferred_element_type=jnp.float32)
        store_slabs(packed * gates, outs, columns)


def call_pack(kernel, slabs, slots, first, base, arrays):
    width = arrays[1].shape[1]
    rows = slabs * slots
    outs = pl.pallas_call(
        functools.partial(kernel, rows, first, base),
        in_specs=[whole(a.shape) for a in arrays],
        out_specs=[whole(s.shape) for s in slab_shapes(slabs, slots, width)],
        out_shape=slab_shapes(slabs, slots, width),
        grid=(1,),
        compiler_params=params(),
        cost_estimate=pl.CostEstimate(
            flops=2 * rows * arrays[1].shape[0] * width,
            bytes_accessed=2 * rows * width + 2 * arrays[1].size,
            transcendentals=0,
        ),
    )(*arrays)
    return to_slabs(outs, slabs, slots)


def resident(value):
    return pltpu.with_memory_space_constraint(value, pltpu.VMEM)


def pre_kernel(part, *refs):
    *slabs, gate_ref, up_ref, pre_gate_ref, pre_up_ref, rows_ref = refs
    gather_slabs(slabs, rows_ref)
    for start in range(0, gate_ref.shape[1], part):
        columns = slice(start, start + part)
        rows = rows_ref[...]
        pre_gate_ref[:, columns] = jnp.dot(rows, gate_ref[:, columns], preferred_element_type=jnp.float32)
        pre_up_ref[:, columns] = jnp.dot(rows, up_ref[:, columns], preferred_element_type=jnp.float32)


def pre_activations(slabs, gate_matrix, up_matrix):
    slabs = from_slabs(slabs)
    count, width = sum(s.shape[0] for s in slabs), slabs[0].shape[1]
    hidden = gate_matrix.shape[1]
    return pl.pallas_call(
        functools.partial(pre_kernel, piece(hidden, 256)),
        in_specs=[VMEM_WHOLE] * (len(slabs) + 2),
        out_specs=[VMEM_WHOLE] * 2,
        out_shape=[jax.ShapeDtypeStruct((count, hidden), jnp.float32)] * 2,
        scratch_shapes=[pltpu.VMEM((count, width), jnp.bfloat16)],
        compiler_params=params(16),
        cost_estimate=pl.CostEstimate(
            flops=4 * count * width * hidden,
            bytes_accessed=4 * width * hidden + 2 * count * width + 8 * count * hidden,
            transcendentals=0,
        ),
        name="pre_activations",
    )(*slabs, resident(gate_matrix), resident(up_matrix))


def hidden_kernel(part, *refs):
    *slabs, down_ref, hidden_ref, rows_ref = refs
    gather_slabs(slabs, rows_ref)
    for start in range(0, down_ref.shape[0], part):
        columns = slice(start, start + part)
        hidden_ref[:, columns] = contract_last(rows_ref[...], down_ref[columns, :])


def hidden_gradient(slabs, down_matrix):
    slabs = from_slabs(slabs)
    count, width = sum(s.shape[0] for s in slabs), slabs[0].shape[1]
    hidden = down_matrix.shape[0]
    return pl.pallas_call(
        functools.partial(hidden_kernel, piece(hidden, 256)),
        in_specs=[VMEM_WHOLE] * (len(slabs) + 1),
        out_specs=VMEM_WHOLE,
        out_shape=jax.ShapeDtypeStruct((count, hidden), jnp.float32),
        scratch_shapes=[pltpu.VMEM((count, width), jnp.bfloat16)],
        compiler_params=params(16),
        cost_estimate=pl.CostEstimate(
            flops=2 * count * width * hidden,
            bytes_accessed=2 * width * hidden + 2 * count * width + 4 * count * hidden,
            transcendentals=0,
        ),
        name="hidden_gradient",
    )(*slabs, resident(down_matrix))


def store_grads(pre_gate, pre_up, hidden_grad, gate_grad, up_grad, columns):
    sigmoid = 1.0 / (1.0 + jnp.exp(-pre_gate))
    both = hidden_grad * sigmoid
    gate_grad[:, columns] = (both * pre_up * (1.0 + pre_gate * (1.0 - sigmoid))).astype(jnp.bfloat16)
    up_grad[:, columns] = (both * pre_gate).astype(jnp.bfloat16)


def store_rows(gate_grad, up_grad, gate_ref, up_ref, outs, column):
    for start in range(0, gate_ref.shape[0], column):
        chosen = slice(start, start + column)
        total = contract_last(gate_grad[...], gate_ref[chosen, :]) + contract_last(
            up_grad[...], up_ref[chosen, :]
        )
        store_slabs(total, outs, chosen)


def gradient_last_kernel(part, column, count_in, *refs):
    slabs, refs = refs[:count_in], refs[count_in:]
    pre_gate_ref, pre_up_ref, down_ref, gate_ref, up_ref, *outs = refs
    *outs, rows_ref, gate_grad, up_grad = outs
    gather_slabs(slabs, rows_ref)
    for start in range(0, gate_ref.shape[1], part):
        columns = slice(start, start + part)
        hidden_grad = contract_last(rows_ref[...], down_ref[columns, :])
        store_grads(
            pre_gate_ref[:, columns], pre_up_ref[:, columns], hidden_grad, gate_grad, up_grad, columns
        )
    store_rows(gate_grad, up_grad, gate_ref, up_ref, outs, column)


def normed_last_kernel(part, column, count_in, *refs):
    slabs, refs = refs[:count_in], refs[count_in:]
    pre_gate_ref, pre_up_ref, hidden_ref, gate_ref, up_ref, *outs = refs
    *outs, rows_ref, gate_grad, up_grad = outs
    gather_slabs(slabs, rows_ref)
    for start in range(0, gate_ref.shape[1], part):
        columns = slice(start, start + part)
        far_gate = jnp.dot(rows_ref[...], gate_ref[:, columns], preferred_element_type=jnp.float32)
        far_up = jnp.dot(rows_ref[...], up_ref[:, columns], preferred_element_type=jnp.float32)
        pre_gate = jnp.concatenate([pre_gate_ref[:, columns], far_gate], axis=0)
        pre_up = jnp.concatenate([pre_up_ref[:, columns], far_up], axis=0)
        store_grads(pre_gate, pre_up, hidden_ref[:, columns], gate_grad, up_grad, columns)
    store_rows(gate_grad, up_grad, gate_ref, up_ref, outs, column)


def call_backward(kernel, slabs, number, slots, given, matrices):
    slabs = from_slabs(slabs)
    count, width = number * slots, slabs[0].shape[1]
    gathered = sum(s.shape[0] for s in slabs)
    hidden = matrices[-1].shape[1]
    shapes = slab_shapes(number, slots, width)
    outs = pl.pallas_call(
        functools.partial(kernel, piece(hidden, 256), piece(width, 256), len(slabs)),
        in_specs=[VMEM_WHOLE] * (len(slabs) + len(given) + len(matrices)),
        out_specs=[VMEM_WHOLE] * len(shapes),
        out_shape=shapes,
        scratch_shapes=[pltpu.VMEM((gathered, width), jnp.bfloat16)]
        + [pltpu.VMEM((count, hidden), jnp.bfloat16)] * 2,
        compiler_params=params(16),
        cost_estimate=pl.CostEstimate(
            flops=6 * count * width * hidden,
            bytes_accessed=6 * width * hidden + 4 * count * width + 8 * count * hidden,
            transcendentals=count * hidden,
        ),
        name="expert_backward",
    )(*slabs, *given, *[resident(m) for m in matrices])
    return to_slabs(outs, number, slots)


def combined(slabs, info_ref, first, x_ref, incoming_of, gain_ref, rows_ref, weighted_ref, put):
    gather_slabs(slabs, rows_ref)
    rows, width = rows_ref.shape
    chosen = one_hot(slot_hits(info_ref, first, rows, 0))
    inverse = inverse_of(x_ref)
    part = piece(width, 512)
    project = None
    for start in range(0, width, part):
        columns = slice(start, start + part)
        normed_grad = lax.dot_general(
            chosen, rows_ref[:, columns], (((0,), (0,)), ((), ())), preferred_element_type=jnp.float32
        )
        weighted = gain_ref[:, columns] * normed_grad
        weighted_ref[:, columns] = weighted
        term = jnp.sum(x_ref[:, columns].astype(jnp.float32) * weighted, axis=1, keepdims=True)
        project = term if project is None else project + term
    factor = inverse * inverse * inverse * (project / width)
    for start in range(0, width, part):
        columns = slice(start, start + part)
        put(
            columns,
            (
                incoming_of(columns).astype(jnp.float32)
                + inverse * weighted_ref[:, columns]
                - x_ref[:, columns].astype(jnp.float32) * factor
            ).astype(jnp.bfloat16),
        )


def relay_kernel(count_in, *refs):
    slabs, refs = refs[:count_in], refs[count_in:]
    flag_ref, info_ref, next_ref, x_ref, incoming_ref, fresh_ref, gain_ref, result_ref, *outs = refs
    *outs, rows_ref, weighted_ref = outs
    rows = rows_ref.shape[0]
    hits = slot_hits(next_ref, TOPK, rows, 0)
    chosen = one_hot(hits)
    gates = slot_gates(hits, next_ref, 3 * TOPK)
    takes_fresh = flag_ref[0] == 0

    def put(columns, value):
        result_ref[:, columns] = value
        passed = jnp.where(takes_fresh, fresh_ref[:, columns], value)
        store_slabs(jnp.dot(chosen, passed, preferred_element_type=jnp.float32) * gates, outs, columns)

    combined(slabs, info_ref, 0, x_ref, lambda c: incoming_ref[:, c], gain_ref, rows_ref, weighted_ref, put)


def final_kernel(count_in, *refs):
    slabs, refs = refs[:count_in], refs[count_in:]
    flag_ref, info_ref, x_ref, arrived_ref, fresh_ref, gain_ref, result_ref, out_ref = refs[:8]
    rows_ref, weighted_ref = refs[8:]
    out_ref[0] = result_ref[...]
    takes_fresh = flag_ref[1] == 0

    def put(columns, value):
        out_ref[1, :, columns] = value

    def incoming_of(columns):
        return jnp.where(takes_fresh, fresh_ref[:, columns], arrived_ref[:, columns])

    combined(slabs, info_ref, TOPK, x_ref, incoming_of, gain_ref, rows_ref, weighted_ref, put)


def call_combine(kernel, slabs, arrays, shapes):
    slabs = from_slabs(slabs)
    count, width = sum(s.shape[0] for s in slabs), slabs[0].shape[1]
    tokens = arrays[-1].shape[0]
    specs = [whole(s.shape) for s in slabs] + [pl.BlockSpec(memory_space=pltpu.SMEM)]
    return pl.pallas_call(
        functools.partial(kernel, len(slabs)),
        in_specs=specs + [whole(a.shape) for a in arrays[1:]],
        out_specs=[whole(s.shape) for s in shapes],
        out_shape=shapes,
        grid=(1,),
        scratch_shapes=[
            pltpu.VMEM((count, width), jnp.bfloat16),
            pltpu.VMEM((shapes[0].shape[-2], width), jnp.float32),
        ],
        compiler_params=params(),
        cost_estimate=pl.CostEstimate(
            flops=4 * count * tokens * width, bytes_accessed=4 * count * width, transcendentals=0
        ),
    )(*slabs, *arrays)


def local(layer_input, entering, fresh, routes, gate_weights, norm_gain, w_gate, w_up, w_down):
    experts = lax.axis_size("expert")
    sections = lax.axis_size("section")
    tokens, width = layer_input.shape[2], layer_input.shape[3]
    slots = max(2, min(tokens, 3 * tokens * TOPK // (2 * experts)))
    half = experts // 2
    here = lax.axis_index("expert")
    section_here = lax.axis_index("section")
    gate_matrix, up_matrix, down_matrix = w_gate[0, 0], w_up[0, 0], w_down[0, 0]
    layer_rows = [layer_input[t, 0] for t in range(TICKS)]
    token_rows = jax.ShapeDtypeStruct((tokens, width), jnp.bfloat16)

    def across(value, k):
        return lax.ppermute(value, "expert", [(i, i ^ k) for i in range(experts)])

    def deal(slabs):
        return [slabs[0]] + [across(slabs[k], k) for k in range(1, len(slabs))]

    def previous(value, k):
        pairs = [
            (s * experts + i, (s - 1) % sections * experts + (i ^ k))
            for s in range(sections)
            for i in range(experts)
        ]
        return lax.ppermute(value, ("section", "expert"), pairs)

    grad_mirror = across(entering[0], half)

    chosen = routes[:, 0].transpose(0, 2, 1)
    expert_ids = jnp.arange(experts, dtype=jnp.int32)
    onehot = chosen[:, :, None, :] == expert_ids[None, None, :, None]
    named = jnp.sum(onehot.astype(jnp.float32), axis=1).astype(jnp.bfloat16)
    order = jnp.arange(tokens, dtype=jnp.int32)
    before = (order[:, None] < order[None, :]).astype(jnp.bfloat16)
    counted = lax.dot_general(
        named, before, (((2,), (0,)), ((), ())), preferred_element_type=jnp.float32
    )
    rank = jnp.sum(jnp.where(onehot, counted[:, None], 0.0), axis=2)
    place = (chosen ^ here).astype(jnp.float32) * slots + rank
    gates = gate_weights[:, 0].transpose(0, 2, 1).astype(jnp.float32)
    info = jnp.concatenate([place, gates], axis=0).reshape(2 * TICKS * TOPK, tokens)
    info_mirror = across(info, half)
    info_next = lax.ppermute(info, "section", [(s, (s + 1) % sections) for s in range(sections)])
    x0_mirror = across(layer_rows[0], half)

    def normed(t, values, given, base):
        return call_pack(pack_normed_kernel, half, slots, TOPK * t, base * slots, [given, values, norm_gain])

    def scaled(values, given, base):
        return call_pack(pack_scaled_kernel, half, slots, 0, base * slots, [given, values])

    scaled0 = deal(scaled(entering[0], info, 0))
    rows0 = deal(normed(0, layer_rows[0], info, 0))
    scaled0 += deal(scaled(grad_mirror, info_mirror, half))
    rows0 += deal(normed(0, x0_mirror, info_mirror, half))
    x1_mirror = across(layer_rows[1], half)

    def deal_all(slabs):
        near = deal(slabs[:half])
        far = []
        for k in range(half, experts):
            far.append(across(slabs[k], k))
        return near + far

    given = [*pre_activations(rows0[:half], gate_matrix, up_matrix)]
    given += [hidden_gradient(scaled0, down_matrix)]
    computed0 = call_backward(
        normed_last_kernel, rows0[half:], experts, slots, given, [gate_matrix, up_matrix]
    )
    returned0 = deal_all(computed0)
    rows1 = deal(normed(1, layer_rows[1], info, 0))
    rows1 += deal(normed(1, x1_mirror, info_mirror, half))

    flags = jnp.stack([section_here, sections - 1 - section_here]).astype(jnp.int32)
    relayed = call_combine(
        relay_kernel,
        returned0,
        [flags, info, info_next, layer_rows[0], entering[0], fresh[0], norm_gain],
        [token_rows] + slab_shapes(experts, slots, width),
    )
    result0 = relayed[0]
    outgoing = to_slabs(relayed[1:], experts, slots)
    scaled1 = [previous(outgoing[k], k) for k in range(half)]
    for k in range(half, experts):
        scaled1.append(previous(outgoing[k], k))
    arrived = previous(result0, 0)
    given = [*pre_activations(rows1, gate_matrix, up_matrix)]
    computed1 = call_backward(
        gradient_last_kernel, scaled1, experts, slots, given, [down_matrix, gate_matrix, up_matrix]
    )
    returned1 = deal_all(computed1)
    (out,) = call_combine(
        final_kernel,
        returned1,
        [flags, info, layer_rows[1], arrived, fresh[0], norm_gain, result0],
        [jax.ShapeDtypeStruct((TICKS, tokens, width), jnp.bfloat16)],
    )
    return out[:, None]


def solution(mesh):
    in_specs = (
        P(None, "section", "expert", None),
        P("section", "expert", None),
        P(None, "expert", None),
        P(None, "section", "expert", None),
        P(None, "section", "expert", None),
        P("section", None),
        P("section", "expert", None, None),
        P("section", "expert", None, None),
        P("section", "expert", None, None),
    )
    out_specs = P(None, "section", "expert", None)

    return jax.shard_map(local, mesh=mesh, in_specs=in_specs, out_specs=out_specs, check_vma=False)
```
